32 devices in a mesh: dp: 8 (over z, y), shard: 4 (over x, core).
Axes of the slice: x: 2, y: 2, z: 4, core: 2. Of those that a mesh axis runs over, the one named last changes fastest.
Arguments:
- tokens: bfloat16 [4096, 768], P(('dp', 'shard')), may hold values from -6 to 6
- cotangent: bfloat16 [4096, 768], P(('dp', 'shard')), may hold values from -6 to 6
- seq_ids: int32 [4096], P(('dp', 'shard')), may hold values from -1 to 127, as said below
- params: float32 [3768320], P(('dp', 'shard')), as said below
- first_moment: float32 [3768320], P(('dp', 'shard')), may hold values from -60 to 60
- second_moment: float32 [3768320], P(('dp', 'shard')), may hold values from 1 to 20
- step_count: int32 [1], replicated, may hold values from 1 to 20
Outputs:
- block_out: bfloat16 [4096, 768], P(('dp', 'shard'))
- grad_input: float32 [4096, 768], P(('dp', 'shard'))
- weight_grads: float32 [3768320], P(('dp', 'shard'))
- new_params: float32 [3768320], P(('dp', 'shard'))
- new_first_moment: float32 [3768320], P(('dp', 'shard'))
- new_second_moment: float32 [3768320], P(('dp', 'shard'))
The draws below stay inside these ranges and needn't reach their ends.
Inputs may be any that keep to these rules, and one draw needn't show every extreme that they name: `seq_ids`: numbering restarts on every device's 128 slots: a device's first slot starts a sequence, consecutive equal numbers form one sequence, live slots come first and the remaining ones are -1. A sequence has at most 128 slots; some device holds exactly one such sequence, and some device has every slot live as a sequence of its own. `params`: entries are laid out as in the first step of the statement.
All inputs are finite; a program needn't handle non-finite values.
Results may differ from the reference program's by a relative error of at most 0.01.
Values may be sent and summed in bfloat16 or wider, within the bound.
A program may use at most 128 MiB of HBM per device.

```python
import math
import jax
import jax.numpy as jnp
from jax import lax

D = 768
HEADS = 24
HEAD_DIM = 64
STATE = 128
KERNEL = 4
STRETCH = 128
TOK_DEV = 128
INNER = 1536
CHANNELS = 1792
PRAW = 3765320
PTOTAL = 3768320
TOKENS = 4096


def draw_seq_ids(key, part):
    blocks = TOKENS // TOK_DEV
    key_live, key_full, key_cut = jax.random.split(key, 3)
    live = jax.random.randint(key_live, (blocks,), TOK_DEV // 4, TOK_DEV + 1)
    chosen = jax.random.randint(key_full, (), 0, blocks)
    half_block = (chosen + 1) % blocks
    single_block = (chosen + 2) % blocks
    block_index = jnp.arange(blocks, dtype=jnp.int32)
    live = jnp.where(block_index == half_block, TOK_DEV // 2, live)
    live = jnp.where(block_index == single_block, TOK_DEV, live)
    live = jnp.where(block_index == chosen, TOK_DEV, live)
    spacing = max(TOK_DEV // 3, 2)
    cuts = (jax.random.randint(key_cut, (blocks, TOK_DEV), 0, spacing) == 0).astype(jnp.int32)
    position = jnp.arange(TOK_DEV, dtype=jnp.int32)
    cuts = jnp.where(position[None, :] == 0, 1, cuts)
    cuts = jnp.where((block_index == single_block)[:, None], 1, cuts)
    cuts = jnp.where((block_index == chosen)[:, None] & (position[None, :] > 0), 0, cuts)
    local_ids = jnp.cumsum(cuts, axis=1) - 1
    local_ids = jnp.where(position[None, :] < live[:, None], local_ids, -1)
    return local_ids.reshape(TOKENS).astype(jnp.int32)


def draw_params(key, part):
    keys = jax.random.split(key, 11)
    main_noise = jax.random.normal(keys[1], (D * (INNER + CHANNELS),), jnp.float32)
    dt_noise = jax.random.normal(keys[2], (D * HEADS,), jnp.float32)
    out_noise = jax.random.normal(keys[9], (INNER * D,), jnp.float32)
    gain_in = jax.random.uniform(keys[0], (D,), jnp.float32, 0.5, 1.5)
    w_main = main_noise * D ** (-0.5)
    w_dt = dt_noise * D ** (-0.5)
    conv_w = jax.random.uniform(keys[3], (KERNEL * CHANNELS,), jnp.float32, -0.6, 0.6)
    conv_b = jax.random.uniform(keys[4], (CHANNELS,), jnp.float32, -0.5, 0.5)
    dt_start = jnp.exp(jax.random.uniform(keys[5], (HEADS,), jnp.float32, -6.9077553, -2.3025851))
    dt_bias = jnp.log(jnp.expm1(dt_start))
    a_log = jax.random.uniform(keys[6], (HEADS,), jnp.float32, 0.0, 2.7725887)
    d_skip = jax.random.uniform(keys[7], (HEADS,), jnp.float32, 0.5, 1.5)
    gain_out = jax.random.uniform(keys[8], (INNER,), jnp.float32, 0.5, 1.5)
    w_out = out_noise * INNER ** (-0.5)
    unused = jax.random.normal(keys[10], (PTOTAL - PRAW,), jnp.float32) * 0.02
    return jnp.concatenate([gain_in, w_main, w_dt, conv_w, conv_b, dt_bias, a_log, d_skip, gain_out, w_out, unused])


def level_of(key, extent, cuts, least, largest):
    loudness = 1.0
    for dim, parts in cuts:
        steps = jax.random.uniform(jax.random.fold_in(jax.random.fold_in(key, 6), dim), (parts,), jnp.float32, least / len(cuts), largest / len(cuts))
        loudness = loudness * jnp.repeat(jnp.exp(steps), extent[dim] // parts).reshape((-1,) + (1,) * (len(extent) - 1 - dim))
    return loudness


def centred(rng, extent, scale, reach, cuts=(), kind=jnp.bfloat16):
    factor_of = level_of(rng, extent, cuts, -0.22, 0.18) if cuts else 1.0
    array = jax.random.normal(rng, extent, jnp.float32) * scale * factor_of
    return jnp.minimum(jnp.maximum(array, -reach), reach).astype(kind)


def setup_inputs(seed: int = 0) -> dict:
    streams_of = jax.random.split(jax.random.key(seed), 8)
    tokens = centred(streams_of[0], (TOKENS, D), 1.0, 6.0, ((0, 32),))
    cotangent = centred(streams_of[1], (TOKENS, D), 1.0, 6.0, ((0, 32),))
    seq_ids = draw_seq_ids(jax.random.fold_in(streams_of[7], 71), 0)
    params = draw_params(jax.random.fold_in(streams_of[7], 71), 0)
    first_moment = centred(streams_of[4], (PTOTAL,), 10.0, 60.0, ((0, 32),), jnp.float32)
    second_moment = jnp.clip(jnp.exp(math.log(20.0) - 2.9957323 * jax.random.uniform(streams_of[5], (PTOTAL,), jnp.float32) ** level_of(streams_of[5], (PTOTAL,), ((0, 32),), -0.2, 0.2)), 1.0, 20.0)
    step_count = jax.random.randint(streams_of[6], (1,), 1, 21).astype(jnp.int32)
    return {"tokens": tokens, "cotangent": cotangent, "seq_ids": seq_ids, "params": params, "first_moment": first_moment, "second_moment": second_moment, "step_count": step_count}


EPS = 1e-05
BETA_ONE = 0.9
BETA_TWO = 0.999
ADAM_EPS = 1e-08
LEARN_RATE = 0.01
WEIGHT_DECAY = 0.1

def matmul(left, right):
    return jnp.dot(left, right, preferred_element_type=jnp.float32)

def over_rows(left, right):
    return lax.dot_general(left, right, (((0,), (0,)), ((), ())), preferred_element_type=jnp.float32)

def against(left, right):
    return lax.dot_general(left, right, (((1,), (1,)), ((), ())), preferred_element_type=jnp.float32)

def unpack(flat):
    shapes = [(D,), (D, INNER + CHANNELS), (D, HEADS), (KERNEL, CHANNELS), (CHANNELS,), (HEADS,), (HEADS,), (HEADS,), (INNER,), (INNER, D)]
    pieces = []
    offset = 0
    for shape in shapes:
        length = math.prod(shape)
        pieces.append(flat[offset:offset + length].reshape(shape))
        offset = offset + length
    return pieces

def pack(pieces, total):
    flat = jnp.concatenate([piece.reshape(-1) for piece in pieces])
    return jnp.concatenate([flat, jnp.zeros((total - flat.shape[0],), flat.dtype)])

def norm_in(inputs, gain):
    scale = lax.rsqrt(lax.optimization_barrier(jnp.mean(inputs * inputs, axis=-1, keepdims=True)) + EPS)
    return inputs * scale * gain

def lag_masks(seq_ids):
    padded = jnp.concatenate([jnp.full((KERNEL - 1,), -3, jnp.int32), seq_ids.astype(jnp.int32)])
    masks = []
    for lag in range(1, KERNEL):
        earlier = padded[KERNEL - 1 - lag:KERNEL - 1 - lag + seq_ids.shape[0]]
        masks.append((earlier == seq_ids).astype(jnp.float32)[:, None])
    return masks

def state_space(values, bmat, cmat, steps_dt, rate, seq_ids):
    rows = values.shape[0]
    number = rows // STRETCH
    seg_blocks = seq_ids.astype(jnp.int32).reshape(number, STRETCH)
    before = jnp.concatenate([jnp.full((1,), -3, jnp.int32), seg_blocks[:-1, -1]])
    places = jnp.arange(STRETCH, dtype=jnp.int32)
    lower = places[:, None] >= places[None, :]

    def advance(state, pieces):
        x_block, b_block, c_block, dt_block, seg_block, prior = pieces
        logs = jnp.cumsum(dt_block * rate, axis=0)
        same = lower & (seg_block[:, None] == seg_block[None, :])
        spans = logs.T[:, :, None] - logs.T[:, None, :]
        factor = jnp.exp(jnp.where(same[None], spans, -1e+30))
        scores = jnp.dot(c_block, b_block.T, precision=lax.Precision.HIGHEST)
        mixing = factor * scores[None] * dt_block.T[:, None, :]
        inside = jnp.einsum('htu,uhp->thp', mixing, x_block, precision=lax.Precision.HIGHEST)
        entering = jnp.exp(logs) * (seg_block == prior).astype(logs.dtype)[:, None]
        carried = jnp.einsum('tn,hnp->thp', c_block, state, precision=lax.Precision.HIGHEST) * entering[:, :, None]
        tail_mask = (seg_block == seg_block[-1]).astype(logs.dtype)[:, None]
        towards = jnp.exp(logs[-1][None, :] - logs) * dt_block * tail_mask
        fresh = jnp.einsum('th,tn,thp->hnp', towards, b_block, x_block, precision=lax.Precision.HIGHEST)
        kept = jnp.exp(logs[-1]) * (seg_block[-1] == prior).astype(logs.dtype)
        return (fresh + kept[:, None, None] * state, inside + carried)
    initial = jnp.zeros((HEADS, STATE, HEAD_DIM), values.dtype)
    inputs = (values.reshape(number, STRETCH, HEADS, HEAD_DIM), bmat.reshape(number, STRETCH, STATE), cmat.reshape(number, STRETCH, STATE), steps_dt.reshape(number, STRETCH, HEADS), seg_blocks, before)
    final_state, outputs = lax.scan(advance, initial, inputs)
    return outputs.reshape(rows, HEADS, HEAD_DIM)

def mixer(proj, dt_raw, conv_weight, conv_bias, dt_bias, a_log, d_skip, gain_out, lag_list, seq_ids):
    rows = proj.shape[0]
    gate = proj[:, :INNER]
    conv_in = proj[:, INNER:]
    convolved = conv_bias + conv_weight[KERNEL - 1] * conv_in
    for lag in range(1, KERNEL):
        shifted = jnp.concatenate([jnp.zeros((lag, conv_in.shape[1]), conv_in.dtype), conv_in[:-lag]])
        convolved = convolved + conv_weight[KERNEL - 1 - lag] * shifted * lag_list[lag - 1]
    active = jax.nn.silu(convolved)
    values = active[:, :INNER].reshape(rows, HEADS, HEAD_DIM)
    bmat = active[:, INNER:INNER + STATE]
    cmat = active[:, INNER + STATE:]
    steps_dt = jax.nn.softplus(dt_raw + dt_bias)
    scanned = state_space(values, bmat, cmat, steps_dt, -jnp.exp(a_log), seq_ids)
    scanned = scanned + d_skip[None, :, None] * values
    gated = scanned.reshape(rows, INNER) * jax.nn.silu(gate)
    scale = lax.rsqrt(lax.optimization_barrier(jnp.mean(gated * gated, axis=-1, keepdims=True)) + EPS)
    return gated * scale * gain_out

def block_pass(tokens, cotangent, seq_ids, weights, total):
    gain_in, w_main, w_dt, conv_w, conv_b, dt_bias, a_log, d_skip, gain_out, w_out = weights
    small = [piece.astype(jnp.float32) for piece in (conv_w, conv_b, dt_bias, a_log, d_skip, gain_out)]
    inputs = tokens.astype(jnp.float32)
    normed_full, norm_back = jax.vjp(norm_in, inputs, gain_in.astype(jnp.float32))
    normed = normed_full.astype(jnp.bfloat16)
    proj = matmul(normed, w_main)
    dt_raw = matmul(normed, w_dt)
    masks = lag_masks(seq_ids)
    mixed_full, mixer_back = jax.vjp(partial_mixer(masks, seq_ids), proj, dt_raw, *small)
    hidden = mixed_full.astype(jnp.bfloat16)
    result = (inputs + matmul(hidden, w_out)).astype(jnp.bfloat16)
    live_cot = jnp.where(seq_ids[:, None] >= 0, cotangent, jnp.zeros_like(cotangent))
    grad_w_out = over_rows(hidden, live_cot)
    grad_hidden = against(live_cot, w_out)
    backward = mixer_back(grad_hidden)
    grad_proj = backward[0].astype(jnp.bfloat16)
    grad_dt = backward[1].astype(jnp.bfloat16)
    grad_w_main = over_rows(normed, grad_proj)
    grad_w_dt = over_rows(normed, grad_dt)
    grad_normed = against(grad_proj, w_main) + against(grad_dt, w_dt)
    grad_x, grad_gain = norm_back(grad_normed)
    grad_input = live_cot.astype(jnp.float32) + grad_x
    flat = pack([grad_gain, grad_w_main, grad_w_dt] + list(backward[2:]) + [grad_w_out], total)
    return (result, grad_input, flat)

def partial_mixer(masks, seq_ids):

    def apply_mixer(proj, dt_raw, conv_weight, conv_bias, dt_bias, a_log, d_skip, gain_out):
        return mixer(proj, dt_raw, conv_weight, conv_bias, dt_bias, a_log, d_skip, gain_out, masks, seq_ids)
    return apply_mixer

def adamw(weight, first, second, grad, step_count):
    steps_done = step_count[0].astype(jnp.float32)
    first_new = BETA_ONE * first + (1.0 - BETA_ONE) * grad
    second_new = BETA_TWO * second + (1.0 - BETA_TWO) * grad * grad
    first_hat = first_new / (1.0 - jnp.power(BETA_ONE, steps_done))
    second_hat = second_new / (1.0 - jnp.power(BETA_TWO, steps_done))
    weight_new = weight - LEARN_RATE * (first_hat / (jnp.sqrt(second_hat) + ADAM_EPS) + WEIGHT_DECAY * weight)
    return (weight_new, first_new, second_new)

def reference(tokens, cotangent, seq_ids, params, first_moment, second_moment, step_count):
    weights = unpack(params.astype(jnp.bfloat16))
    blocks = TOKENS // TOK_DEV

    def one_block(summed, pieces):
        token_block, cot_block, seg_block = pieces
        result, grad_input, flat = block_pass(token_block, cot_block, seg_block, weights, PTOTAL)
        return (summed + flat, (result, grad_input))
    start_sum = jnp.zeros((PTOTAL,), jnp.float32)
    summed, (results, grads_in) = lax.scan(one_block, start_sum, (tokens.reshape(blocks, TOK_DEV, D), cotangent.reshape(blocks, TOK_DEV, D), seq_ids.reshape(blocks, TOK_DEV)))
    new_weight, new_first, new_second = adamw(params, first_moment, second_moment, summed, step_count)
    return (results.reshape(TOKENS, D), grads_in.reshape(TOKENS, D), summed, new_weight, new_first, new_second)
```

```python
import functools
import math

import jax
import jax.numpy as jnp
from jax import lax
from jax.experimental import pallas as pl
from jax.experimental.pallas import tpu as pltpu
from jax.sharding import PartitionSpec as P

D = 768
HEADS = 24
HEAD_DIM = 64
STATE = 128
KERNEL = 4
STRETCH = 128
INNER = 1536
CHANNELS = 1792
LANES = 128
CUTS = 4
MESH = pl.DeviceIdType.MESH
PACKED = D + D * (INNER + CHANNELS) + D * HEADS + (KERNEL + 1) * CHANNELS + 3 * HEADS + INNER + INNER * D


EPS = 1e-05
BETA_ONE = 0.9
BETA_TWO = 0.999
ADAM_EPS = 1e-08
LEARN_RATE = 0.01
WEIGHT_DECAY = 0.1


def matmul(left, right):
    return jnp.dot(left, right, preferred_element_type=jnp.float32)


def over_rows(left, right):
    return lax.dot_general(
        left, right, (((0,), (0,)), ((), ())), preferred_element_type=jnp.float32
    )


def against(left, right):
    return lax.dot_general(
        left, right, (((1,), (1,)), ((), ())), preferred_element_type=jnp.float32
    )


def unpack(flat):
    shapes = [
        (D,),
        (D, INNER + CHANNELS),
        (D, HEADS),
        (KERNEL, CHANNELS),
        (CHANNELS,),
        (HEADS,),
        (HEADS,),
        (HEADS,),
        (INNER,),
        (INNER, D),
    ]
    pieces = []
    offset = 0
    for shape in shapes:
        length = math.prod(shape)
        pieces.append(flat[offset : offset + length].reshape(shape))
        offset = offset + length
    return pieces


ROWS_GAIN = D // LANES
ROWS_MAIN = D * (INNER + CHANNELS) // LANES
START_SMALL = ROWS_GAIN + ROWS_MAIN
START_OUT = (PACKED - INNER * D) // LANES
SHIFT = (PACKED - INNER * D) % LANES
ROWS_OUT = INNER * D // LANES
ROWS_SMALL = START_OUT + 1 - START_SMALL
WIDE = (INNER + CHANNELS) // LANES
THIN = D // LANES


def pack_kernel(gain_ref, small_ref, normed_ref, proj_ref, hidden_ref, cot_ref, out_ref, main, tail):
    main[0:ROWS_GAIN, :] = gain_ref[...]
    main[START_SMALL : START_OUT, :] = small_ref[0 : ROWS_SMALL - 1, :]
    tail[7:8, :] = small_ref[ROWS_SMALL - 1 : ROWS_SMALL, :]
    tail[8 + ROWS_OUT :, :] = jnp.zeros((tail.shape[0] - 8 - ROWS_OUT, LANES), jnp.float32)
    for pair in range(WIDE // 2):
        both = over_rows(normed_ref[...], proj_ref[:, pair * 2 * LANES : (pair + 1) * 2 * LANES])
        for side in range(2):
            main[pl.ds(ROWS_GAIN + 2 * pair + side, D, stride=WIDE), :] = both[
                :, side * LANES : (side + 1) * LANES
            ]
    for pair in range(THIN // 2):
        both = over_rows(hidden_ref[...], cot_ref[:, pair * 2 * LANES : (pair + 1) * 2 * LANES])
        for side in range(2):
            part = pltpu.roll(both[:, side * LANES : (side + 1) * LANES], SHIFT, 1)
            tail[pl.ds(8 + 2 * pair + side, INNER, stride=THIN), :] = part
    edge = START_OUT // 16 * 16

    def cast_main(step, carry):
        place = pl.multiple_of(step * 32, 32)
        out_ref[pl.ds(place, 32), :] = main[pl.ds(place, 32), :].astype(jnp.bfloat16)
        return carry

    lax.fori_loop(0, edge // 32, cast_main, 0)
    early = lax.broadcasted_iota(jnp.int32, (8, LANES), 1) < SHIFT
    seam = jnp.where(early, tail[7:15, :], tail[8:16, :])
    out_ref[edge : edge + 16, :] = jnp.concatenate([main[edge : edge + 8, :], seam], 0).astype(
        jnp.bfloat16
    )
    early_two = lax.broadcasted_iota(jnp.int32, (16, LANES), 1) < SHIFT

    def cast_tail(step, carry):
        place = pl.multiple_of(step * 16, 16)
        block = tail[pl.ds(pl.multiple_of(place + 16, 8), 16), :]
        before = tail[pl.ds(pl.multiple_of(place + 8, 8), 16), :]
        joined = jnp.concatenate([before[7:8], block[:15]], 0)
        out_ref[pl.ds(pl.multiple_of(edge + 16 + place, 16), 16), :] = jnp.where(
            early_two, joined, block
        ).astype(jnp.bfloat16)
        return carry

    lax.fori_loop(0, (out_ref.shape[0] - edge - 16) // 16, cast_tail, 0)


def pack_all(gain, small, normed, proj, hidden, cot, rows):
    vmem = pl.BlockSpec(memory_space=pltpu.VMEM)
    return pl.pallas_call(
        pack_kernel,
        out_shape=jax.ShapeDtypeStruct((rows, LANES), jnp.bfloat16),
        in_specs=[vmem] * 6,
        out_specs=vmem,
        scratch_shapes=[
            pltpu.VMEM((START_OUT, LANES), jnp.float32),
            pltpu.VMEM((rows - START_OUT + 16, LANES), jnp.float32),
        ],
        compiler_params=pltpu.CompilerParams(vmem_limit_bytes=48 * 1024 * 1024),
    )(gain, small, normed, proj, hidden, cot)


def scatter_kernel(grid, cuts, data, out, send_sem, recv_sem, *refs):
    deep, tall, wide = grid
    dp, shard = lax.axis_index("dp"), lax.axis_index("shard")
    z, y = lax.div(dp, tall), lax.rem(dp, tall)
    x, c = lax.div(shard, 2), lax.rem(shard, 2)

    def place(z, y, x, c):
        return (z * tall + y, x * 2 + c)

    xs = [lax.rem(x + j, wide) for j in range(1, wide)]
    ys = [lax.rem(y + j, tall) for j in range(1, tall)]
    zs = [lax.rem(z + j, deep) for j in range(1, deep)]
    to_x = [place(z, y, p, c) for p in xs]
    to_y = [place(z, p, x, c) for p in ys]
    to_z = [place(p, y, x, c) for p in zs]
    partner = place(z, y, x, 1 - c)
    everyone = [partner] + to_x + to_y + to_z
    barrier = pltpu.get_barrier_semaphore()
    for peer in everyone:
        pl.semaphore_signal(barrier, inc=1, device_id=peer, device_id_type=MESH)
    pl.semaphore_wait(barrier, len(everyone))

    sent = []

    def push(chunk, number, src, dst, peer):
        copy = pltpu.make_async_remote_copy(
            src_ref=src,
            dst_ref=dst,
            send_sem=send_sem.at[chunk, number],
            recv_sem=recv_sem.at[chunk, number],
            device_id=peer,
            device_id_type=MESH,
        )
        copy.start()
        sent.append(copy)
        return copy

    def total(parts):
        value = parts[0].astype(jnp.float32)
        for part in parts[1:]:
            value = value + part.astype(jnp.float32)
        return value

    first_x, first_y, first_z = 1, wide, wide + tall - 1
    chunks = [refs[i * 7 : i * 7 + 7] for i in range(len(cuts))]
    flights = []
    for k, (start, size) in enumerate(cuts):
        src = data.at[:, :, :, 1 - c, start : start + size]
        flights.append([push(k, 0, src, chunks[k][0], partner)])
    for k, (start, size) in enumerate(cuts):
        got, acc, got_one = chunks[k][:3]
        for copy in flights[k]:
            copy.wait_recv()

        def add(step, carry):
            zi, rest = lax.div(step, tall * wide), lax.rem(step, tall * wide)
            yi, xi = lax.div(rest, wide), lax.rem(rest, wide)
            mine = data[zi, yi, xi, c, start : start + size, :]
            acc[zi, yi, xi] = total([mine, got[zi, yi, xi]]).astype(jnp.bfloat16)
            return carry

        lax.fori_loop(0, deep * tall * wide, add, 0)
        flights[k] = []
        if k % 2 == 0:
            for j, p in enumerate(xs):
                flights[k].append(push(k, first_x + j, acc.at[:, :, p], got_one.at[j], to_x[j]))
        else:
            for j, p in enumerate(ys):
                flights[k].append(push(k, first_y + j, acc.at[:, p], got_one.at[j], to_y[j]))
    for k, (start, size) in enumerate(cuts):
        got, acc, got_one, acc_two, got_two = chunks[k][:5]
        for copy in flights[k]:
            copy.wait_recv()
        other = tall if k % 2 == 0 else wide

        def add(step, carry):
            zi, oi = lax.div(step, other), lax.rem(step, other)
            mine = acc[zi, oi, x] if k % 2 == 0 else acc[zi, y, oi]
            parts = [mine] + [got_one[j, zi, oi] for j in range(got_one.shape[0])]
            acc_two[zi, oi] = total(parts).astype(jnp.bfloat16)
            return carry

        lax.fori_loop(0, deep * other, add, 0)
        flights[k] = []
        if k % 2 == 0:
            for j, p in enumerate(ys):
                flights[k].append(push(k, first_y + j, acc_two.at[:, p], got_two.at[j], to_y[j]))
        else:
            for j, p in enumerate(xs):
                flights[k].append(push(k, first_x + j, acc_two.at[:, p], got_two.at[j], to_x[j]))
    for k, (start, size) in enumerate(cuts):
        acc_two, got_two, acc_three, got_three = chunks[k][3:]
        for copy in flights[k]:
            copy.wait_recv()
        mine = y if k % 2 == 0 else x

        def add(zi, carry):
            parts = [acc_two[zi, mine]] + [got_two[j, zi] for j in range(got_two.shape[0])]
            acc_three[zi] = total(parts).astype(jnp.bfloat16)
            return carry

        lax.fori_loop(0, deep, add, 0)
        flights[k] = []
        for j, p in enumerate(zs):
            flights[k].append(push(k, first_z + j, acc_three.at[p], got_three.at[j], to_z[j]))
    for k, (start, size) in enumerate(cuts):
        acc_three, got_three = chunks[k][5:]
        for copy in flights[k]:
            copy.wait_recv()
        parts = [acc_three[z]] + [got_three[j] for j in range(deep - 1)]
        out[start : start + size, :] = total(parts)
    for copy in sent:
        copy.wait_send()


def scatter_sum(flat, group_count, wide_count, rows):
    wide = group_count // 2
    tall = wide if wide_count % wide == 0 else 1
    deep = wide_count // tall
    step = -(-rows // (CUTS * 16)) * 16
    cuts = [(start, min(step, rows - start)) for start in range(0, rows, step)]
    scratch = []
    for k, (start, size) in enumerate(cuts):
        lead, other = (wide, tall) if k % 2 == 0 else (tall, wide)
        for shape in (
            (deep, tall, wide),
            (deep, tall, wide),
            (lead - 1, deep, other),
            (deep, other),
            (other - 1, deep),
            (deep,),
            (deep - 1,),
        ):
            scratch.append(pltpu.VMEM((*shape, size, LANES), jnp.bfloat16))
    peers = wide + tall + deep - 2
    sems = pltpu.SemaphoreType.DMA((len(cuts), peers))
    vmem = pl.BlockSpec(memory_space=pltpu.VMEM)
    return pl.pallas_call(
        functools.partial(scatter_kernel, (deep, tall, wide), cuts),
        out_shape=jax.ShapeDtypeStruct((rows, LANES), jnp.float32),
        in_specs=[vmem],
        out_specs=vmem,
        scratch_shapes=[sems, sems] + scratch,
        compiler_params=pltpu.CompilerParams(
            collective_id=0, has_side_effects=True, vmem_limit_bytes=56 * 1024 * 1024
        ),
    )(flat.reshape(deep, tall, wide, 2, rows, LANES))


def norm_in(inputs, gain):
    scale = lax.rsqrt(jnp.mean(inputs * inputs, axis=-1, keepdims=True) + EPS)
    return inputs * scale * gain


def lag_masks(seq_ids):
    padded = jnp.concatenate([jnp.full((KERNEL - 1,), -3, jnp.int32), seq_ids])
    masks = []
    for lag in range(1, KERNEL):
        earlier = padded[KERNEL - 1 - lag : KERNEL - 1 - lag + seq_ids.shape[0]]
        masks.append((earlier == seq_ids).astype(jnp.float32)[:, None])
    return masks


def state_space(values, bmat, cmat, steps_dt, rate, seq_ids):
    rows = values.shape[0]
    number = rows // STRETCH
    seg_blocks = seq_ids.reshape(number, STRETCH)
    before = jnp.concatenate([jnp.full((1,), -3, jnp.int32), seg_blocks[:-1, -1]])
    places = jnp.arange(STRETCH, dtype=jnp.int32)
    lower = places[:, None] >= places[None, :]

    def advance(state, pieces):
        x_block, b_block, c_block, dt_block, seg_block, prior = pieces
        logs = jnp.cumsum(dt_block * rate, axis=0)
        same = lower & (seg_block[:, None] == seg_block[None, :])
        spans = logs.T[:, :, None] - logs.T[:, None, :]
        factor = jnp.exp(jnp.where(same[None], spans, -1e30))
        scores = jnp.dot(c_block, b_block.T, precision=lax.Precision.HIGHEST)
        mixing = factor * scores[None] * dt_block.T[:, None, :]
        inside = jnp.einsum("htu,uhp->thp", mixing, x_block, precision=lax.Precision.HIGHEST)
        entering = jnp.exp(logs) * (seg_block == prior).astype(logs.dtype)[:, None]
        carried = (
            jnp.einsum("tn,hnp->thp", c_block, state, precision=lax.Precision.HIGHEST)
            * entering[:, :, None]
        )
        tail_mask = (seg_block == seg_block[-1]).astype(logs.dtype)[:, None]
        towards = jnp.exp(logs[-1][None, :] - logs) * dt_block * tail_mask
        fresh = jnp.einsum(
            "th,tn,thp->hnp", towards, b_block, x_block, precision=lax.Precision.HIGHEST
        )
        kept = jnp.exp(logs[-1]) * (seg_block[-1] == prior).astype(logs.dtype)
        return (fresh + kept[:, None, None] * state, inside + carried)

    initial = jnp.zeros((HEADS, STATE, HEAD_DIM), values.dtype)
    inputs = (
        values.reshape(number, STRETCH, HEADS, HEAD_DIM),
        bmat.reshape(number, STRETCH, STATE),
        cmat.reshape(number, STRETCH, STATE),
        steps_dt.reshape(number, STRETCH, HEADS),
        seg_blocks,
        before,
    )
    final_state, outputs = lax.scan(advance, initial, inputs)
    return outputs.reshape(rows, HEADS, HEAD_DIM)


def mixer(
    proj, dt_raw, conv_weight, conv_bias, dt_bias, a_log, d_skip, gain_out, lag_list, seq_ids
):
    rows = proj.shape[0]
    gate = proj[:, :INNER]
    conv_in = proj[:, INNER:]
    convolved = conv_bias + conv_weight[KERNEL - 1] * conv_in
    for lag in range(1, KERNEL):
        shifted = jnp.concatenate(
            [jnp.zeros((lag, conv_in.shape[1]), conv_in.dtype), conv_in[:-lag]]
        )
        convolved = convolved + conv_weight[KERNEL - 1 - lag] * shifted * lag_list[lag - 1]
    active = jax.nn.silu(convolved)
    values = active[:, :INNER].reshape(rows, HEADS, HEAD_DIM)
    bmat = active[:, INNER : INNER + STATE]
    cmat = active[:, INNER + STATE :]
    steps_dt = jax.nn.softplus(dt_raw + dt_bias)
    scanned = state_space(values, bmat, cmat, steps_dt, -jnp.exp(a_log), seq_ids)
    scanned = scanned + d_skip[None, :, None] * values
    gated = scanned.reshape(rows, INNER) * jax.nn.silu(gate)
    scale = lax.rsqrt(jnp.mean(gated * gated, axis=-1, keepdims=True) + EPS)
    return gated * scale * gain_out


def partial_mixer(masks, seq_ids):

    def apply_mixer(proj, dt_raw, conv_weight, conv_bias, dt_bias, a_log, d_skip, gain_out):
        return mixer(
            proj, dt_raw, conv_weight, conv_bias, dt_bias, a_log, d_skip, gain_out, masks, seq_ids
        )

    return apply_mixer


def block_pass(tokens, cotangent, seq_ids, weights, total):
    gain_in, w_main, w_dt, conv_w, conv_b, dt_bias, a_log, d_skip, gain_out, w_out = weights
    small = [
        piece.astype(jnp.float32) for piece in (conv_w, conv_b, dt_bias, a_log, d_skip, gain_out)
    ]
    inputs = tokens.astype(jnp.float32)
    normed_full, norm_back = jax.vjp(norm_in, inputs, gain_in.astype(jnp.float32))
    normed = normed_full.astype(jnp.bfloat16)
    proj = matmul(normed, w_main)
    dt_raw = matmul(normed, w_dt)
    masks = lag_masks(seq_ids)
    mixed_full, mixer_back = jax.vjp(partial_mixer(masks, seq_ids), proj, dt_raw, *small)
    hidden = mixed_full.astype(jnp.bfloat16)
    result = (inputs + matmul(hidden, w_out)).astype(jnp.bfloat16)
    live_cot = jnp.where(seq_ids[:, None] >= 0, cotangent, jnp.zeros_like(cotangent))
    grad_hidden = against(live_cot, w_out)
    backward = mixer_back(grad_hidden)
    grad_proj = backward[0].astype(jnp.bfloat16)
    grad_dt = backward[1].astype(jnp.bfloat16)
    grad_w_dt = over_rows(normed, grad_dt)
    grad_normed = against(grad_proj, w_main) + against(grad_dt, w_dt)
    grad_x, grad_gain = norm_back(grad_normed)
    grad_input = live_cot.astype(jnp.float32) + grad_x
    small_flat = jnp.concatenate([piece.reshape(-1) for piece in [grad_w_dt] + list(backward[2:])])
    small_flat = jnp.pad(small_flat, (0, ROWS_SMALL * LANES - small_flat.shape[0]))
    flat = pack_all(
        grad_gain.reshape(ROWS_GAIN, LANES),
        small_flat.reshape(ROWS_SMALL, LANES),
        normed,
        grad_proj,
        hidden,
        live_cot,
        total // LANES,
    )
    return (result, grad_input, flat)


def adamw(weight, first, second, grad, step_count):
    steps_done = step_count[0].astype(jnp.float32)
    first_new = BETA_ONE * first + (1.0 - BETA_ONE) * grad
    second_new = BETA_TWO * second + (1.0 - BETA_TWO) * grad * grad
    first_hat = first_new / (1.0 - jnp.power(BETA_ONE, steps_done))
    second_hat = second_new / (1.0 - jnp.power(BETA_TWO, steps_done))
    weight_new = weight - LEARN_RATE * (
        first_hat / (jnp.sqrt(second_hat) + ADAM_EPS) + WEIGHT_DECAY * weight
    )
    return (weight_new, first_new, second_new)


def per_device(tokens, cotangent, seq_ids, params, first_moment, second_moment, step_count):
    width = params.shape[0]
    rounded = params.astype(jnp.bfloat16)
    whole = lax.all_gather(rounded, ("dp", "shard"), axis=0, tiled=True)
    weights = unpack(whole)
    result, grad_input, flat = block_pass(tokens, cotangent, seq_ids, weights, whole.shape[0])
    owned = scatter_sum(flat, lax.axis_size("shard"), lax.axis_size("dp"), width // LANES)
    owned = owned.reshape(width)
    new_weight, new_first, new_second = adamw(
        params, first_moment, second_moment, owned, step_count
    )
    return (result, grad_input, owned, new_weight, new_first, new_second)


def solution(mesh):
    return jax.shard_map(
        per_device,
        mesh=mesh,
        in_specs=(
            P(("dp", "shard"), None),
            P(("dp", "shard"), None),
            P(("dp", "shard")),
            P(("dp", "shard")),
            P(("dp", "shard")),
            P(("dp", "shard")),
            P(),
        ),
        out_specs=(
            P(("dp", "shard"), None),
            P(("dp", "shard"), None),
            P(("dp", "shard")),
            P(("dp", "shard")),
            P(("dp", "shard")),
            P(("dp", "shard")),
        ),
        check_vma=False,
    )
```

```python
import functools
import math

import jax
import jax.numpy as jnp
from jax import lax
from jax.experimental import pallas as pl
from jax.experimental.pallas import tpu as pltpu
from jax.sharding import PartitionSpec as P

D = 768
HEADS = 24
HEAD_DIM = 64
STATE = 128
KERNEL = 4
STRETCH = 128
INNER = 1536
CHANNELS = 1792
LANES = 128
CUTS = 8
SPAN = 256
MESH = pl.DeviceIdType.MESH
PACKED = D + D * (INNER + CHANNELS) + D * HEADS + (KERNEL + 1) * CHANNELS + 3 * HEADS + INNER + INNER * D


EPS = 1e-05
BETA_ONE = 0.9
BETA_TWO = 0.999
ADAM_EPS = 1e-08
LEARN_RATE = 0.01
WEIGHT_DECAY = 0.1


def matmul(left, right):
    return jnp.dot(left, right, preferred_element_type=jnp.float32)


def over_rows(left, right):
    return lax.dot_general(
        left, right, (((0,), (0,)), ((), ())), preferred_element_type=jnp.float32
    )


def against(left, right):
    return lax.dot_general(
        left, right, (((1,), (1,)), ((), ())), preferred_element_type=jnp.float32
    )


ROWS_GAIN = D // LANES
ROWS_MAIN = D * (INNER + CHANNELS) // LANES
START_SMALL = ROWS_GAIN + ROWS_MAIN
START_OUT = (PACKED - INNER * D) // LANES
SHIFT = (PACKED - INNER * D) % LANES
ROWS_OUT = INNER * D // LANES
ROWS_SMALL = START_OUT + 1 - START_SMALL
WIDE = (INNER + CHANNELS) // LANES
THIN = D // LANES


def in_spans(total, body):
    def step(number, carry):
        body(pl.multiple_of(number * SPAN, SPAN), SPAN)
        return carry

    whole = total // SPAN
    lax.fori_loop(0, whole, step, 0)
    if total % SPAN:
        body(whole * SPAN, total - whole * SPAN)


def pack_kernel(gain_ref, small_ref, normed_ref, proj_ref, hidden_ref, cot_ref, out_ref, main, tail):
    main[0:ROWS_GAIN, :] = gain_ref[...]
    main[START_SMALL : START_OUT, :] = small_ref[0 : ROWS_SMALL - 1, :]
    tail[7:8, :] = small_ref[ROWS_SMALL - 1 : ROWS_SMALL, :]
    tail[8 + ROWS_OUT :, :] = jnp.zeros((tail.shape[0] - 8 - ROWS_OUT, LANES), jnp.float32)
    for pair in range(WIDE // 2):
        both = over_rows(normed_ref[...], proj_ref[:, pair * 2 * LANES : (pair + 1) * 2 * LANES])
        for side in range(2):
            main[pl.ds(ROWS_GAIN + 2 * pair + side, D, stride=WIDE), :] = both[
                :, side * LANES : (side + 1) * LANES
            ]
    for pair in range(THIN // 2):
        both = over_rows(hidden_ref[...], cot_ref[:, pair * 2 * LANES : (pair + 1) * 2 * LANES])
        for side in range(2):
            part = pltpu.roll(both[:, side * LANES : (side + 1) * LANES], SHIFT, 1)
            tail[pl.ds(8 + 2 * pair + side, INNER, stride=THIN), :] = part
    edge = START_OUT // 16 * 16

    def cast_main(place, size):
        out_ref[pl.ds(place, size), :] = main[pl.ds(place, size), :].astype(jnp.bfloat16)

    in_spans(edge, cast_main)
    early = lax.broadcasted_iota(jnp.int32, (8, LANES), 1) < SHIFT
    seam = jnp.where(early, tail[7:15, :], tail[8:16, :])
    out_ref[edge : edge + 16, :] = jnp.concatenate([main[edge : edge + 8, :], seam], 0).astype(
        jnp.bfloat16
    )

    def cast_tail(place, size):
        block = tail[pl.ds(place + 16, size), :]
        before = tail[pl.ds(place + 8, size), :]
        joined = jnp.concatenate([before[7:8], block[: size - 1]], 0)
        lanes = lax.broadcasted_iota(jnp.int32, (size, LANES), 1)
        out_ref[pl.ds(edge + 16 + place, size), :] = jnp.where(
            lanes < SHIFT, joined, block
        ).astype(jnp.bfloat16)

    in_spans(out_ref.shape[0] - edge - 16, cast_tail)


def pack_all(gain, small, normed, proj, hidden, cot, rows):
    vmem = pl.BlockSpec(memory_space=pltpu.VMEM)
    return pl.pallas_call(
        pack_kernel,
        out_shape=jax.ShapeDtypeStruct((rows, LANES), jnp.bfloat16),
        in_specs=[vmem] * 6,
        out_specs=vmem,
        scratch_shapes=[
            pltpu.VMEM((START_OUT, LANES), jnp.float32),
            pltpu.VMEM((rows - START_OUT + 16, LANES), jnp.float32),
        ],
        compiler_params=pltpu.CompilerParams(vmem_limit_bytes=48 * 1024 * 1024),
    )(gain, small, normed, proj, hidden, cot)


def scatter_kernel(grid, cuts, data, out, send_sem, recv_sem, *refs):
    deep, tall, wide = grid
    dp, shard = lax.axis_index("dp"), lax.axis_index("shard")
    z, y = lax.div(dp, tall), lax.rem(dp, tall)
    x, c = lax.div(shard, 2), lax.rem(shard, 2)

    def place(z, y, x, c):
        return (z * tall + y, x * 2 + c)

    xs = [lax.rem(x + j, wide) for j in range(1, wide)]
    ys = [lax.rem(y + j, tall) for j in range(1, tall)]
    zs = [lax.rem(z + j, deep) for j in range(1, deep)]
    to_x = [place(z, y, p, c) for p in xs]
    to_y = [place(z, p, x, c) for p in ys]
    to_z = [place(p, y, x, c) for p in zs]
    partner = place(z, y, x, 1 - c)
    everyone = [partner] + to_x + to_y + to_z
    barrier = pltpu.get_barrier_semaphore()
    for peer in everyone:
        pl.semaphore_signal(barrier, inc=1, device_id=peer, device_id_type=MESH)
    pl.semaphore_wait(barrier, len(everyone))

    sent = []

    def push(chunk, number, src, dst, peer):
        copy = pltpu.make_async_remote_copy(
            src_ref=src,
            dst_ref=dst,
            send_sem=send_sem.at[chunk, number],
            recv_sem=recv_sem.at[chunk, number],
            device_id=peer,
            device_id_type=MESH,
        )
        copy.start()
        sent.append(copy)
        return copy

    def total(parts):
        value = parts[0].astype(jnp.float32)
        for part in parts[1:]:
            value = value + part.astype(jnp.float32)
        return value

    first_x, first_y, first_z = 1, wide, wide + tall - 1
    chunks = [refs[i * 7 : i * 7 + 7] for i in range(len(cuts))]
    flights = []
    for k, (start, size) in enumerate(cuts):
        src = data.at[:, :, :, 1 - c, start : start + size]
        flights.append([push(k, 0, src, chunks[k][0], partner)])
    for k, (start, size) in enumerate(cuts):
        got, acc, got_one = chunks[k][:3]
        for copy in flights[k]:
            copy.wait_recv()

        def add(step, carry):
            zi, rest = lax.div(step, tall * wide), lax.rem(step, tall * wide)
            yi, xi = lax.div(rest, wide), lax.rem(rest, wide)
            mine = data[zi, yi, xi, c, start : start + size, :]
            acc[zi, yi, xi] = total([mine, got[zi, yi, xi]]).astype(jnp.bfloat16)
            return carry

        lax.fori_loop(0, deep * tall * wide, add, 0)
        flights[k] = []
        if k % 2 == 0:
            for j, p in enumerate(xs):
                flights[k].append(push(k, first_x + j, acc.at[:, :, p], got_one.at[j], to_x[j]))
        else:
            for j, p in enumerate(ys):
                flights[k].append(push(k, first_y + j, acc.at[:, p], got_one.at[j], to_y[j]))
    for k, (start, size) in enumerate(cuts):
        got, acc, got_one, acc_two, got_two = chunks[k][:5]
        for copy in flights[k]:
            copy.wait_recv()
        other = tall if k % 2 == 0 else wide

        def add(step, carry):
            zi, oi = lax.div(step, other), lax.rem(step, other)
            mine = acc[zi, oi, x] if k % 2 == 0 else acc[zi, y, oi]
            parts = [mine] + [got_one[j, zi, oi] for j in range(got_one.shape[0])]
            acc_two[zi, oi] = total(parts).astype(jnp.bfloat16)
            return carry

        lax.fori_loop(0, deep * other, add, 0)
        flights[k] = []
        if k % 2 == 0:
            for j, p in enumerate(ys):
                flights[k].append(push(k, first_y + j, acc_two.at[:, p], got_two.at[j], to_y[j]))
        else:
            for j, p in enumerate(xs):
                flights[k].append(push(k, first_x + j, acc_two.at[:, p], got_two.at[j], to_x[j]))
    for k, (start, size) in enumerate(cuts):
        acc_two, got_two, acc_three, got_three = chunks[k][3:]
        for copy in flights[k]:
            copy.wait_recv()
        mine = y if k % 2 == 0 else x

        def add(zi, carry):
            parts = [acc_two[zi, mine]] + [got_two[j, zi] for j in range(got_two.shape[0])]
            acc_three[zi] = total(parts).astype(jnp.bfloat16)
            return carry

        lax.fori_loop(0, deep, add, 0)
        flights[k] = []
        for j, p in enumerate(zs):
            flights[k].append(push(k, first_z + j, acc_three.at[p], got_three.at[j], to_z[j]))
    for k, (start, size) in enumerate(cuts):
        acc_three, got_three = chunks[k][5:]
        for copy in flights[k]:
            copy.wait_recv()
        parts = [acc_three[z]] + [got_three[j] for j in range(deep - 1)]
        out[start : start + size, :] = total(parts)
    for copy in sent:
        copy.wait_send()


def scatter_sum(flat, group_count, wide_count, rows):
    wide = group_count // 2
    tall = wide if wide_count % wide == 0 else 1
    deep = wide_count // tall
    step = -(-rows // (CUTS * 16)) * 16
    cuts = [(start, min(step, rows - start)) for start in range(0, rows, step)]
    scratch = []
    for k, (start, size) in enumerate(cuts):
        lead, other = (wide, tall) if k % 2 == 0 else (tall, wide)
        for shape in (
            (deep, tall, wide),
            (deep, tall, wide),
            (lead - 1, deep, other),
            (deep, other),
            (other - 1, deep),
            (deep,),
            (deep - 1,),
        ):
            scratch.append(pltpu.VMEM((*shape, size, LANES), jnp.bfloat16))
    peers = wide + tall + deep - 2
    sems = pltpu.SemaphoreType.DMA((len(cuts), peers))
    vmem = pl.BlockSpec(memory_space=pltpu.VMEM)
    return pl.pallas_call(
        functools.partial(scatter_kernel, (deep, tall, wide), cuts),
        out_shape=jax.ShapeDtypeStruct((rows, LANES), jnp.float32),
        in_specs=[vmem],
        out_specs=vmem,
        scratch_shapes=[sems, sems] + scratch,
        compiler_params=pltpu.CompilerParams(
            collective_id=0, has_side_effects=True, vmem_limit_bytes=56 * 1024 * 1024
        ),
    )(flat.reshape(deep, tall, wide, 2, rows, LANES))


def gather_kernel(grid, cuts, own, out, send_sem, recv_sem):
    deep, tall, wide = grid
    dp, shard = lax.axis_index("dp"), lax.axis_index("shard")
    z, y = lax.div(dp, tall), lax.rem(dp, tall)
    x, c = lax.div(shard, 2), lax.rem(shard, 2)

    def place(z, y, x, c):
        return (z * tall + y, x * 2 + c)

    to_x = [place(z, y, lax.rem(x + j, wide), c) for j in range(1, wide)]
    to_y = [place(z, lax.rem(y + j, tall), x, c) for j in range(1, tall)]
    to_z = [place(lax.rem(z + j, deep), y, x, c) for j in range(1, deep)]
    partner = place(z, y, x, 1 - c)
    everyone = [partner] + to_x + to_y + to_z
    barrier = pltpu.get_barrier_semaphore()
    for peer in everyone:
        pl.semaphore_signal(barrier, inc=1, device_id=peer, device_id_type=MESH)
    pl.semaphore_wait(barrier, len(everyone))

    sent = []

    def push(chunk, number, src, dst, peers):
        started = []
        for j, peer in enumerate(peers):
            copy = pltpu.make_async_remote_copy(
                src_ref=src,
                dst_ref=dst,
                send_sem=send_sem.at[chunk, number + j],
                recv_sem=recv_sem.at[chunk, number + j],
                device_id=peer,
                device_id_type=MESH,
            )
            copy.start()
            started.append(copy)
        sent.extend(started)
        return started

    first_x, first_y, first_z = 1, wide, wide + tall - 1
    flights = []
    for k, (start, size) in enumerate(cuts):
        rows = pl.ds(start, size)
        flights.append(push(k, first_z, own.at[rows], out.at[z, y, x, c, rows], to_z))
    out[z, y, x, c] = own[...]
    for k, (start, size) in enumerate(cuts):
        rows = pl.ds(start, size)
        for copy in flights[k]:
            copy.wait_recv()
        line = out.at[:, y, x, c, rows]
        if k % 2 == 0:
            flights[k] = push(k, first_y, line, line, to_y)
        else:
            flights[k] = push(k, first_x, line, line, to_x)
    for k, (start, size) in enumerate(cuts):
        rows = pl.ds(start, size)
        for copy in flights[k]:
            copy.wait_recv()
        if k % 2 == 0:
            sheet = out.at[:, :, x, c, rows]
            flights[k] = push(k, first_x, sheet, sheet, to_x)
        else:
            sheet = out.at[:, y, :, c, rows]
            flights[k] = push(k, first_y, sheet, sheet, to_y)
    for k, (start, size) in enumerate(cuts):
        for copy in flights[k]:
            copy.wait_recv()
        cube = out.at[:, :, :, c, pl.ds(start, size)]
        flights[k] = push(k, 0, cube, cube, [partner])
    for flight in flights:
        for copy in flight:
            copy.wait_recv()
    for copy in sent:
        copy.wait_send()


def gather_rows(own, group_count, wide_count):
    rows = own.shape[0]
    wide = group_count // 2
    tall = wide if wide_count % wide == 0 else 1
    deep = wide_count // tall
    step = -(-rows // (CUTS * 16)) * 16
    cuts = [(start, min(step, rows - start)) for start in range(0, rows, step)]
    sems = pltpu.SemaphoreType.DMA((len(cuts), wide + tall + deep - 2))
    vmem = pl.BlockSpec(memory_space=pltpu.VMEM)
    whole = pl.pallas_call(
        functools.partial(gather_kernel, (deep, tall, wide), cuts),
        out_shape=jax.ShapeDtypeStruct((deep, tall, wide, 2, rows, LANES), jnp.bfloat16),
        in_specs=[vmem],
        out_specs=vmem,
        scratch_shapes=[sems, sems],
        compiler_params=pltpu.CompilerParams(
            collective_id=1, has_side_effects=True, vmem_limit_bytes=32 * 1024 * 1024
        ),
    )(own)
    return whole.reshape(wide_count * group_count * rows, LANES)


def unpack_kernel(rows_ref, main_ref, out_ref, main, tail):
    edge = START_OUT // 16 * 16

    def widen(place, size):
        main[pl.ds(place, size), :] = rows_ref[pl.ds(place, size), :].astype(jnp.float32)

    in_spans(main.shape[0], widen)

    def widen_tail(place, size):
        block = rows_ref[pl.ds(edge + place, size), :].astype(jnp.float32)
        tail[pl.ds(place, size), :] = pltpu.roll(block, LANES - SHIFT, 1)

    in_spans(tail.shape[0], widen_tail)
    for j in range(WIDE):
        main_ref[:, j * LANES : (j + 1) * LANES] = main[
            pl.ds(ROWS_GAIN + j, D, stride=WIDE), :
        ].astype(jnp.bfloat16)
    early = lax.broadcasted_iota(jnp.int32, (INNER, LANES), 1) < LANES - SHIFT
    base = START_OUT - edge
    for j in range(THIN):
        here = tail[pl.ds(base + j, INNER, stride=THIN), :]
        after = tail[pl.ds(base + j + 1, INNER, stride=THIN), :]
        out_ref[:, j * LANES : (j + 1) * LANES] = jnp.where(early, here, after).astype(
            jnp.bfloat16
        )


def unpack(rows):
    w_main, w_out = unpack_wide(rows)
    gain_in = rows[:ROWS_GAIN].reshape(D)
    flat = rows[START_SMALL : START_SMALL + ROWS_SMALL].reshape(-1)
    shapes = [(D, HEADS), (KERNEL, CHANNELS), (CHANNELS,), (HEADS,), (HEADS,), (HEADS,), (INNER,)]
    pieces = []
    offset = 0
    for shape in shapes:
        length = math.prod(shape)
        pieces.append(flat[offset : offset + length].reshape(shape))
        offset = offset + length
    return [gain_in, w_main] + pieces + [w_out]


def unpack_wide(rows):
    vmem = pl.BlockSpec(memory_space=pltpu.VMEM)
    edge = START_OUT // 16 * 16
    return pl.pallas_call(
        unpack_kernel,
        out_shape=(
            jax.ShapeDtypeStruct((D, INNER + CHANNELS), jnp.bfloat16),
            jax.ShapeDtypeStruct((INNER, D), jnp.bfloat16),
        ),
        in_specs=[vmem],
        out_specs=(vmem, vmem),
        scratch_shapes=[
            pltpu.VMEM((-(-START_SMALL // 32) * 32, LANES), jnp.float32),
            pltpu.VMEM(((rows.shape[0] - edge) // 32 * 32, LANES), jnp.float32),
        ],
        compiler_params=pltpu.CompilerParams(vmem_limit_bytes=48 * 1024 * 1024),
    )(rows)


def norm_in(inputs, gain):
    scale = lax.rsqrt(jnp.mean(inputs * inputs, axis=-1, keepdims=True) + EPS)
    return inputs * scale * gain


def lag_masks(seq_ids):
    padded = jnp.concatenate([jnp.full((KERNEL - 1,), -3, jnp.int32), seq_ids])
    masks = []
    for lag in range(1, KERNEL):
        earlier = padded[KERNEL - 1 - lag : KERNEL - 1 - lag + seq_ids.shape[0]]
        masks.append((earlier == seq_ids).astype(jnp.float32)[:, None])
    return masks


def one_stretch(values, bmat, cmat, steps_dt, rate, seq_ids):
    places = jnp.arange(values.shape[0], dtype=jnp.int32)
    same = (places[:, None] >= places[None, :]) & (seq_ids[:, None] == seq_ids[None, :])
    logs = jnp.cumsum(steps_dt * rate, axis=0).T
    spans = logs[:, :, None] - logs[:, None, :]
    factor = jnp.exp(jnp.where(same[None], spans, -1e30))
    scores = jnp.dot(cmat, bmat.T, precision=lax.Precision.HIGH)
    mixing = factor * scores[None] * steps_dt.T[:, None, :]
    return jnp.einsum("htu,uhp->thp", mixing, values, precision=lax.Precision.HIGH)


def state_space(values, bmat, cmat, steps_dt, rate, seq_ids):
    rows = values.shape[0]
    number = rows // STRETCH
    if number == 1:
        return one_stretch(values, bmat, cmat, steps_dt, rate, seq_ids)
    seg_blocks = seq_ids.reshape(number, STRETCH)
    before = jnp.concatenate([jnp.full((1,), -3, jnp.int32), seg_blocks[:-1, -1]])
    places = jnp.arange(STRETCH, dtype=jnp.int32)
    lower = places[:, None] >= places[None, :]

    def advance(state, pieces):
        x_block, b_block, c_block, dt_block, seg_block, prior = pieces
        logs = jnp.cumsum(dt_block * rate, axis=0)
        same = lower & (seg_block[:, None] == seg_block[None, :])
        spans = logs.T[:, :, None] - logs.T[:, None, :]
        factor = jnp.exp(jnp.where(same[None], spans, -1e30))
        scores = jnp.dot(c_block, b_block.T, precision=lax.Precision.HIGHEST)
        mixing = factor * scores[None] * dt_block.T[:, None, :]
        inside = jnp.einsum("htu,uhp->thp", mixing, x_block, precision=lax.Precision.HIGHEST)
        entering = jnp.exp(logs) * (seg_block == prior).astype(logs.dtype)[:, None]
        carried = (
            jnp.einsum("tn,hnp->thp", c_block, state, precision=lax.Precision.HIGHEST)
            * entering[:, :, None]
        )
        tail_mask = (seg_block == seg_block[-1]).astype(logs.dtype)[:, None]
        towards = jnp.exp(logs[-1][None, :] - logs) * dt_block * tail_mask
        fresh = jnp.einsum(
            "th,tn,thp->hnp", towards, b_block, x_block, precision=lax.Precision.HIGHEST
        )
        kept = jnp.exp(logs[-1]) * (seg_block[-1] == prior).astype(logs.dtype)
        return (fresh + kept[:, None, None] * state, inside + carried)

    initial = jnp.zeros((HEADS, STATE, HEAD_DIM), values.dtype)
    inputs = (
        values.reshape(number, STRETCH, HEADS, HEAD_DIM),
        bmat.reshape(number, STRETCH, STATE),
        cmat.reshape(number, STRETCH, STATE),
        steps_dt.reshape(number, STRETCH, HEADS),
        seg_blocks,
        before,
    )
    final_state, outputs = lax.scan(advance, initial, inputs)
    return outputs.reshape(rows, HEADS, HEAD_DIM)


def mixer(
    proj, dt_raw, conv_weight, conv_bias, dt_bias, a_log, d_skip, gain_out, lag_list, seq_ids
):
    rows = proj.shape[0]
    gate = proj[:, :INNER]
    conv_in = proj[:, INNER:]
    convolved = conv_bias + conv_weight[KERNEL - 1] * conv_in
    for lag in range(1, KERNEL):
        shifted = jnp.concatenate(
            [jnp.zeros((lag, conv_in.shape[1]), conv_in.dtype), conv_in[:-lag]]
        )
        convolved = convolved + conv_weight[KERNEL - 1 - lag] * shifted * lag_list[lag - 1]
    active = jax.nn.silu(convolved)
    values = active[:, :INNER].reshape(rows, HEADS, HEAD_DIM)
    bmat = active[:, INNER : INNER + STATE]
    cmat = active[:, INNER + STATE :]
    steps_dt = jax.nn.softplus(dt_raw + dt_bias)
    scanned = state_space(values, bmat, cmat, steps_dt, -jnp.exp(a_log), seq_ids)
    scanned = scanned + d_skip[None, :, None] * values
    gated = scanned.reshape(rows, INNER) * jax.nn.silu(gate)
    scale = lax.rsqrt(jnp.mean(gated * gated, axis=-1, keepdims=True) + EPS)
    return gated * scale * gain_out


def partial_mixer(masks, seq_ids):

    def apply_mixer(proj, dt_raw, conv_weight, conv_bias, dt_bias, a_log, d_skip, gain_out):
        return mixer(
            proj, dt_raw, conv_weight, conv_bias, dt_bias, a_log, d_skip, gain_out, masks, seq_ids
        )

    return apply_mixer


def block_pass(tokens, cotangent, seq_ids, weights, total):
    gain_in, w_main, w_dt, conv_w, conv_b, dt_bias, a_log, d_skip, gain_out, w_out = weights
    small = [
        piece.astype(jnp.float32) for piece in (conv_w, conv_b, dt_bias, a_log, d_skip, gain_out)
    ]
    inputs = tokens.astype(jnp.float32)
    normed_full, norm_back = jax.vjp(norm_in, inputs, gain_in.astype(jnp.float32))
    normed = normed_full.astype(jnp.bfloat16)
    proj = matmul(normed, w_main)
    dt_raw = matmul(normed, w_dt)
    masks = lag_masks(seq_ids)
    mixed_full, mixer_back = jax.vjp(partial_mixer(masks, seq_ids), proj, dt_raw, *small)
    hidden = mixed_full.astype(jnp.bfloat16)
    result = (inputs + matmul(hidden, w_out)).astype(jnp.bfloat16)
    live_cot = jnp.where(seq_ids[:, None] >= 0, cotangent, jnp.zeros_like(cotangent))
    grad_hidden = against(live_cot, w_out)
    backward = mixer_back(grad_hidden)
    grad_proj = backward[0].astype(jnp.bfloat16)
    grad_dt = backward[1].astype(jnp.bfloat16)
    grad_w_dt = over_rows(normed, grad_dt)
    grad_normed = against(grad_proj, w_main) + against(grad_dt, w_dt)
    grad_x, grad_gain = norm_back(grad_normed)
    grad_input = live_cot.astype(jnp.float32) + grad_x
    small_flat = jnp.concatenate([piece.reshape(-1) for piece in [grad_w_dt] + list(backward[2:])])
    small_flat = jnp.pad(small_flat, (0, ROWS_SMALL * LANES - small_flat.shape[0]))
    flat = pack_all(
        grad_gain.reshape(ROWS_GAIN, LANES),
        small_flat.reshape(ROWS_SMALL, LANES),
        normed,
        grad_proj,
        hidden,
        live_cot,
        total // LANES,
    )
    return (result, grad_input, flat)


def adamw(weight, first, second, grad, step_count):
    steps_done = step_count[0].astype(jnp.float32)
    first_new = BETA_ONE * first + (1.0 - BETA_ONE) * grad
    second_new = BETA_TWO * second + (1.0 - BETA_TWO) * grad * grad
    first_hat = first_new / (1.0 - jnp.power(BETA_ONE, steps_done))
    second_hat = second_new / (1.0 - jnp.power(BETA_TWO, steps_done))
    weight_new = weight - LEARN_RATE * (
        first_hat / (jnp.sqrt(second_hat) + ADAM_EPS) + WEIGHT_DECAY * weight
    )
    return (weight_new, first_new, second_new)


def per_device(tokens, cotangent, seq_ids, params, first_moment, second_moment, step_count):
    width = params.shape[0]
    rounded = params.astype(jnp.bfloat16)
    own = rounded.reshape(width // LANES, LANES)
    whole = gather_rows(own, lax.axis_size("shard"), lax.axis_size("dp"))
    weights = unpack(whole)
    result, grad_input, flat = block_pass(tokens, cotangent, seq_ids, weights, whole.size)
    owned = scatter_sum(flat, lax.axis_size("shard"), lax.axis_size("dp"), width // LANES)
    owned = owned.reshape(width)
    new_weight, new_first, new_second = adamw(
        params, first_moment, second_moment, owned, step_count
    )
    return (result, grad_input, owned, new_weight, new_first, new_second)


def solution(mesh):
    return jax.shard_map(
        per_device,
        mesh=mesh,
        in_specs=(
            P(("dp", "shard"), None),
            P(("dp", "shard"), None),
            P(("dp", "shard")),
            P(("dp", "shard")),
            P(("dp", "shard")),
            P(("dp", "shard")),
            P(),
        ),
        out_specs=(
            P(("dp", "shard"), None),
            P(("dp", "shard"), None),
            P(("dp", "shard")),
            P(("dp", "shard")),
            P(("dp", "shard")),
            P(("dp", "shard")),
        ),
        check_vma=False,
    )
```

```python
import functools
import math

import jax
import jax.numpy as jnp
from jax import lax
from jax.experimental import pallas as pl
from jax.experimental.pallas import tpu as pltpu
from jax.sharding import PartitionSpec as P

D = 768
HEADS = 24
HEAD_DIM = 64
STATE = 128
KERNEL = 4
STRETCH = 128
INNER = 1536
CHANNELS = 1792
LANES = 128
CUTS = 8
LAG = 2
SPAN = 256
MESH = pl.DeviceIdType.MESH
PACKED = D + D * (INNER + CHANNELS) + D * HEADS + (KERNEL + 1) * CHANNELS + 3 * HEADS + INNER + INNER * D


EPS = 1e-05
BETA_ONE = 0.9
BETA_TWO = 0.999
ADAM_EPS = 1e-08
LEARN_RATE = 0.01
WEIGHT_DECAY = 0.1


def matmul(left, right):
    return jnp.dot(left, right, preferred_element_type=jnp.float32)


def over_rows(left, right):
    return lax.dot_general(
        left, right, (((0,), (0,)), ((), ())), preferred_element_type=jnp.float32
    )


def against(left, right):
    return lax.dot_general(
        left, right, (((1,), (1,)), ((), ())), preferred_element_type=jnp.float32
    )


ROWS_GAIN = D // LANES
ROWS_MAIN = D * (INNER + CHANNELS) // LANES
START_SMALL = ROWS_GAIN + ROWS_MAIN
START_OUT = (PACKED - INNER * D) // LANES
SHIFT = (PACKED - INNER * D) % LANES
ROWS_OUT = INNER * D // LANES
ROWS_SMALL = START_OUT + 1 - START_SMALL
WIDE = (INNER + CHANNELS) // LANES
THIN = D // LANES


def in_spans(total, body):
    def step(number, carry):
        body(pl.multiple_of(number * SPAN, SPAN), SPAN)
        return carry

    whole = total // SPAN
    lax.fori_loop(0, whole, step, 0)
    if total % SPAN:
        body(whole * SPAN, total - whole * SPAN)


def pack_kernel(gain_ref, small_ref, normed_ref, proj_ref, hidden_ref, cot_ref, out_ref, main, tail):
    main[0:ROWS_GAIN, :] = gain_ref[...]
    main[START_SMALL : START_OUT, :] = small_ref[0 : ROWS_SMALL - 1, :]
    tail[7:8, :] = small_ref[ROWS_SMALL - 1 : ROWS_SMALL, :]
    tail[8 + ROWS_OUT :, :] = jnp.zeros((tail.shape[0] - 8 - ROWS_OUT, LANES), jnp.float32)
    for pair in range(WIDE // 2):
        both = over_rows(normed_ref[...], proj_ref[:, pair * 2 * LANES : (pair + 1) * 2 * LANES])
        for side in range(2):
            main[pl.ds(ROWS_GAIN + 2 * pair + side, D, stride=WIDE), :] = both[
                :, side * LANES : (side + 1) * LANES
            ]
    for pair in range(THIN // 2):
        both = over_rows(hidden_ref[...], cot_ref[:, pair * 2 * LANES : (pair + 1) * 2 * LANES])
        for side in range(2):
            part = pltpu.roll(both[:, side * LANES : (side + 1) * LANES], SHIFT, 1)
            tail[pl.ds(8 + 2 * pair + side, INNER, stride=THIN), :] = part
    edge = START_OUT // 16 * 16

    def cast_main(place, size):
        out_ref[pl.ds(place, size), :] = main[pl.ds(place, size), :].astype(jnp.bfloat16)

    in_spans(edge, cast_main)
    early = lax.broadcasted_iota(jnp.int32, (8, LANES), 1) < SHIFT
    seam = jnp.where(early, tail[7:15, :], tail[8:16, :])
    out_ref[edge : edge + 16, :] = jnp.concatenate([main[edge : edge + 8, :], seam], 0).astype(
        jnp.bfloat16
    )

    def cast_tail(place, size):
        block = tail[pl.ds(place + 16, size), :]
        before = tail[pl.ds(place + 8, size), :]
        joined = jnp.concatenate([before[7:8], block[: size - 1]], 0)
        lanes = lax.broadcasted_iota(jnp.int32, (size, LANES), 1)
        out_ref[pl.ds(edge + 16 + place, size), :] = jnp.where(
            lanes < SHIFT, joined, block
        ).astype(jnp.bfloat16)

    in_spans(out_ref.shape[0] - edge - 16, cast_tail)


def pack_all(gain, small, normed, proj, hidden, cot, rows):
    vmem = pl.BlockSpec(memory_space=pltpu.VMEM)
    return pl.pallas_call(
        pack_kernel,
        out_shape=jax.ShapeDtypeStruct((rows, LANES), jnp.bfloat16),
        in_specs=[vmem] * 6,
        out_specs=vmem,
        scratch_shapes=[
            pltpu.VMEM((START_OUT, LANES), jnp.float32),
            pltpu.VMEM((rows - START_OUT + 16, LANES), jnp.float32),
        ],
        compiler_params=pltpu.CompilerParams(vmem_limit_bytes=48 * 1024 * 1024),
    )(gain, small, normed, proj, hidden, cot)


def in_waves(stages, count):
    for wave in range(count + LAG * (len(stages) - 1)):
        for number, stage in enumerate(stages):
            if 0 <= wave - LAG * number < count:
                stage(wave - LAG * number)


def scatter_kernel(grid, cuts, data, out, send_sem, recv_sem, *refs):
    deep, tall, wide = grid
    dp, shard = lax.axis_index("dp"), lax.axis_index("shard")
    z, y = lax.div(dp, tall), lax.rem(dp, tall)
    x, c = lax.div(shard, 2), lax.rem(shard, 2)

    def place(z, y, x, c):
        return (z * tall + y, x * 2 + c)

    xs = [lax.rem(x + j, wide) for j in range(1, wide)]
    ys = [lax.rem(y + j, tall) for j in range(1, tall)]
    zs = [lax.rem(z + j, deep) for j in range(1, deep)]
    to_x = [place(z, y, p, c) for p in xs]
    to_y = [place(z, p, x, c) for p in ys]
    to_z = [place(p, y, x, c) for p in zs]
    partner = place(z, y, x, 1 - c)
    everyone = [partner] + to_x + to_y + to_z
    barrier = pltpu.get_barrier_semaphore()
    for peer in everyone:
        pl.semaphore_signal(barrier, inc=1, device_id=peer, device_id_type=MESH)
    pl.semaphore_wait(barrier, len(everyone))

    sent = []

    def push(chunk, number, src, dst, peer):
        copy = pltpu.make_async_remote_copy(
            src_ref=src,
            dst_ref=dst,
            send_sem=send_sem.at[chunk, number],
            recv_sem=recv_sem.at[chunk, number],
            device_id=peer,
            device_id_type=MESH,
        )
        copy.start()
        sent.append(copy)
        return copy

    def total(parts):
        value = parts[0].astype(jnp.float32)
        for part in parts[1:]:
            value = value + part.astype(jnp.float32)
        return value

    first_x, first_y, first_z = 1, wide, wide + tall - 1
    chunks = [refs[i * 7 : i * 7 + 7] for i in range(len(cuts))]
    flights = []
    for k, (start, size) in enumerate(cuts):
        src = data.at[:, :, :, 1 - c, start : start + size]
        flights.append([push(k, 0, src, chunks[k][0], partner)])
    def stage_one(k):
        start, size = cuts[k]
        got, acc, got_one = chunks[k][:3]
        for copy in flights[k]:
            copy.wait_recv()

        def add(step, carry):
            zi, rest = lax.div(step, tall * wide), lax.rem(step, tall * wide)
            yi, xi = lax.div(rest, wide), lax.rem(rest, wide)
            mine = data[zi, yi, xi, c, start : start + size, :]
            acc[zi, yi, xi] = total([mine, got[zi, yi, xi]]).astype(jnp.bfloat16)
            return carry

        lax.fori_loop(0, deep * tall * wide, add, 0)
        flights[k] = []
        if k % 2 == 0:
            for j, p in enumerate(xs):
                flights[k].append(push(k, first_x + j, acc.at[:, :, p], got_one.at[j], to_x[j]))
        else:
            for j, p in enumerate(ys):
                flights[k].append(push(k, first_y + j, acc.at[:, p], got_one.at[j], to_y[j]))
    def stage_two(k):
        start, size = cuts[k]
        got, acc, got_one, acc_two, got_two = chunks[k][:5]
        for copy in flights[k]:
            copy.wait_recv()
        other = tall if k % 2 == 0 else wide

        def add(step, carry):
            zi, oi = lax.div(step, other), lax.rem(step, other)
            mine = acc[zi, oi, x] if k % 2 == 0 else acc[zi, y, oi]
            parts = [mine] + [got_one[j, zi, oi] for j in range(got_one.shape[0])]
            acc_two[zi, oi] = total(parts).astype(jnp.bfloat16)
            return carry

        lax.fori_loop(0, deep * other, add, 0)
        flights[k] = []
        if k % 2 == 0:
            for j, p in enumerate(ys):
                flights[k].append(push(k, first_y + j, acc_two.at[:, p], got_two.at[j], to_y[j]))
        else:
            for j, p in enumerate(xs):
                flights[k].append(push(k, first_x + j, acc_two.at[:, p], got_two.at[j], to_x[j]))
    def stage_three(k):
        start, size = cuts[k]
        acc_two, got_two, acc_three, got_three = chunks[k][3:]
        for copy in flights[k]:
            copy.wait_recv()
        mine = y if k % 2 == 0 else x

        def add(zi, carry):
            parts = [acc_two[zi, mine]] + [got_two[j, zi] for j in range(got_two.shape[0])]
            acc_three[zi] = total(parts).astype(jnp.bfloat16)
            return carry

        lax.fori_loop(0, deep, add, 0)
        flights[k] = []
        for j, p in enumerate(zs):
            flights[k].append(push(k, first_z + j, acc_three.at[p], got_three.at[j], to_z[j]))
    def stage_four(k):
        start, size = cuts[k]
        acc_three, got_three = chunks[k][5:]
        for copy in flights[k]:
            copy.wait_recv()
        parts = [acc_three[z]] + [got_three[j] for j in range(deep - 1)]
        out[start : start + size, :] = total(parts)

    in_waves((stage_one, stage_two, stage_three, stage_four), len(cuts))
    for copy in sent:
        copy.wait_send()


def scatter_sum(flat, group_count, wide_count, rows):
    wide = group_count // 2
    tall = wide if wide_count % wide == 0 else 1
    deep = wide_count // tall
    step = -(-rows // (CUTS * 16)) * 16
    cuts = [(start, min(step, rows - start)) for start in range(0, rows, step)]
    scratch = []
    for k, (start, size) in enumerate(cuts):
        lead, other = (wide, tall) if k % 2 == 0 else (tall, wide)
        for shape in (
            (deep, tall, wide),
            (deep, tall, wide),
            (lead - 1, deep, other),
            (deep, other),
            (other - 1, deep),
            (deep,),
            (deep - 1,),
        ):
            scratch.append(pltpu.VMEM((*shape, size, LANES), jnp.bfloat16))
    peers = wide + tall + deep - 2
    sems = pltpu.SemaphoreType.DMA((len(cuts), peers))
    vmem = pl.BlockSpec(memory_space=pltpu.VMEM)
    return pl.pallas_call(
        functools.partial(scatter_kernel, (deep, tall, wide), cuts),
        out_shape=jax.ShapeDtypeStruct((rows, LANES), jnp.float32),
        in_specs=[vmem],
        out_specs=vmem,
        scratch_shapes=[sems, sems] + scratch,
        compiler_params=pltpu.CompilerParams(
            collective_id=0, has_side_effects=True, vmem_limit_bytes=56 * 1024 * 1024
        ),
    )(flat.reshape(deep, tall, wide, 2, rows, LANES))


def gather_kernel(grid, cuts, own, out, send_sem, recv_sem):
    deep, tall, wide = grid
    dp, shard = lax.axis_index("dp"), lax.axis_index("shard")
    z, y = lax.div(dp, tall), lax.rem(dp, tall)
    x, c = lax.div(shard, 2), lax.rem(shard, 2)

    def place(z, y, x, c):
        return (z * tall + y, x * 2 + c)

    to_x = [place(z, y, lax.rem(x + j, wide), c) for j in range(1, wide)]
    to_y = [place(z, lax.rem(y + j, tall), x, c) for j in range(1, tall)]
    to_z = [place(lax.rem(z + j, deep), y, x, c) for j in range(1, deep)]
    partner = place(z, y, x, 1 - c)
    everyone = [partner] + to_x + to_y + to_z
    barrier = pltpu.get_barrier_semaphore()
    for peer in everyone:
        pl.semaphore_signal(barrier, inc=1, device_id=peer, device_id_type=MESH)
    pl.semaphore_wait(barrier, len(everyone))

    sent = []

    def push(chunk, number, src, dst, peers):
        started = []
        for j, peer in enumerate(peers):
            copy = pltpu.make_async_remote_copy(
                src_ref=src,
                dst_ref=dst,
                send_sem=send_sem.at[chunk, number + j],
                recv_sem=recv_sem.at[chunk, number + j],
                device_id=peer,
                device_id_type=MESH,
            )
            copy.start()
            started.append(copy)
        sent.extend(started)
        return started

    first_x, first_y, first_z = 1, wide, wide + tall - 1
    flights = []
    for k, (start, size) in enumerate(cuts):
        rows = pl.ds(start, size)
        flights.append(push(k, first_z, own.at[rows], out.at[z, y, x, c, rows], to_z))
    out[z, y, x, c] = own[...]
    def stage_one(k):
        start, size = cuts[k]
        rows = pl.ds(start, size)
        for copy in flights[k]:
            copy.wait_recv()
        line = out.at[:, y, x, c, rows]
        if k % 2 == 0:
            flights[k] = push(k, first_y, line, line, to_y)
        else:
            flights[k] = push(k, first_x, line, line, to_x)
    def stage_two(k):
        start, size = cuts[k]
        rows = pl.ds(start, size)
        for copy in flights[k]:
            copy.wait_recv()
        if k % 2 == 0:
            sheet = out.at[:, :, x, c, rows]
            flights[k] = push(k, first_x, sheet, sheet, to_x)
        else:
            sheet = out.at[:, y, :, c, rows]
            flights[k] = push(k, first_y, sheet, sheet, to_y)
    def stage_three(k):
        start, size = cuts[k]
        for copy in flights[k]:
            copy.wait_recv()
        cube = out.at[:, :, :, c, pl.ds(start, size)]
        flights[k] = push(k, 0, cube, cube, [partner])
    in_waves((stage_one, stage_two, stage_three), len(cuts))
    for flight in flights:
        for copy in flight:
            copy.wait_recv()
    for copy in sent:
        copy.wait_send()


def gather_rows(own, group_count, wide_count):
    rows = own.shape[0]
    wide = group_count // 2
    tall = wide if wide_count % wide == 0 else 1
    deep = wide_count // tall
    step = -(-rows // (CUTS * 16)) * 16
    cuts = [(start, min(step, rows - start)) for start in range(0, rows, step)]
    sems = pltpu.SemaphoreType.DMA((len(cuts), wide + tall + deep - 2))
    vmem = pl.BlockSpec(memory_space=pltpu.VMEM)
    whole = pl.pallas_call(
        functools.partial(gather_kernel, (deep, tall, wide), cuts),
        out_shape=jax.ShapeDtypeStruct((deep, tall, wide, 2, rows, LANES), jnp.bfloat16),
        in_specs=[vmem],
        out_specs=vmem,
        scratch_shapes=[sems, sems],
        compiler_params=pltpu.CompilerParams(
            collective_id=1, has_side_effects=True, vmem_limit_bytes=32 * 1024 * 1024
        ),
    )(own)
    return whole.reshape(wide_count * group_count * rows, LANES)


def unpack_kernel(rows_ref, main_ref, out_ref, main, tail):
    edge = START_OUT // 16 * 16

    def widen(place, size):
        main[pl.ds(place, size), :] = rows_ref[pl.ds(place, size), :].astype(jnp.float32)

    in_spans(main.shape[0], widen)

    def widen_tail(place, size):
        block = rows_ref[pl.ds(edge + place, size), :].astype(jnp.float32)
        tail[pl.ds(place, size), :] = pltpu.roll(block, LANES - SHIFT, 1)

    in_spans(tail.shape[0], widen_tail)
    for j in range(WIDE):
        main_ref[:, j * LANES : (j + 1) * LANES] = main[
            pl.ds(ROWS_GAIN + j, D, stride=WIDE), :
        ].astype(jnp.bfloat16)
    early = lax.broadcasted_iota(jnp.int32, (INNER, LANES), 1) < LANES - SHIFT
    base = START_OUT - edge
    for j in range(THIN):
        here = tail[pl.ds(base + j, INNER, stride=THIN), :]
        after = tail[pl.ds(base + j + 1, INNER, stride=THIN), :]
        out_ref[:, j * LANES : (j + 1) * LANES] = jnp.where(early, here, after).astype(
            jnp.bfloat16
        )


def unpack(rows):
    w_main, w_out = unpack_wide(rows)
    gain_in = rows[:ROWS_GAIN].reshape(D)
    flat = rows[START_SMALL : START_SMALL + ROWS_SMALL].reshape(-1)
    shapes = [(D, HEADS), (KERNEL, CHANNELS), (CHANNELS,), (HEADS,), (HEADS,), (HEADS,), (INNER,)]
    pieces = []
    offset = 0
    for shape in shapes:
        length = math.prod(shape)
        pieces.append(flat[offset : offset + length].reshape(shape))
        offset = offset + length
    return [gain_in, w_main] + pieces + [w_out]


def unpack_wide(rows):
    vmem = pl.BlockSpec(memory_space=pltpu.VMEM)
    edge = START_OUT // 16 * 16
    return pl.pallas_call(
        unpack_kernel,
        out_shape=(
            jax.ShapeDtypeStruct((D, INNER + CHANNELS), jnp.bfloat16),
            jax.ShapeDtypeStruct((INNER, D), jnp.bfloat16),
        ),
        in_specs=[vmem],
        out_specs=(vmem, vmem),
        scratch_shapes=[
            pltpu.VMEM((-(-START_SMALL // 32) * 32, LANES), jnp.float32),
            pltpu.VMEM(((rows.shape[0] - edge) // 32 * 32, LANES), jnp.float32),
        ],
        compiler_params=pltpu.CompilerParams(vmem_limit_bytes=48 * 1024 * 1024),
    )(rows)


def norm_in(inputs, gain):
    scale = lax.rsqrt(jnp.mean(inputs * inputs, axis=-1, keepdims=True) + EPS)
    return inputs * scale * gain


def lag_masks(seq_ids):
    padded = jnp.concatenate([jnp.full((KERNEL - 1,), -3, jnp.int32), seq_ids])
    masks = []
    for lag in range(1, KERNEL):
        earlier = padded[KERNEL - 1 - lag : KERNEL - 1 - lag + seq_ids.shape[0]]
        masks.append((earlier == seq_ids).astype(jnp.float32)[:, None])
    return masks


def one_stretch(values, bmat, cmat, steps_dt, rate, seq_ids):
    places = jnp.arange(values.shape[0], dtype=jnp.int32)
    same = (places[:, None] >= places[None, :]) & (seq_ids[:, None] == seq_ids[None, :])
    logs = jnp.cumsum(steps_dt * rate, axis=0).T
    spans = logs[:, :, None] - logs[:, None, :]
    factor = jnp.exp(jnp.where(same[None], spans, -1e30))
    scores = jnp.dot(cmat, bmat.T, precision=lax.Precision.HIGH)
    mixing = factor * scores[None] * steps_dt.T[:, None, :]
    return jnp.einsum("htu,uhp->thp", mixing, values, precision=lax.Precision.HIGH)


def state_space(values, bmat, cmat, steps_dt, rate, seq_ids):
    rows = values.shape[0]
    number = rows // STRETCH
    if number == 1:
        return one_stretch(values, bmat, cmat, steps_dt, rate, seq_ids)
    seg_blocks = seq_ids.reshape(number, STRETCH)
    before = jnp.concatenate([jnp.full((1,), -3, jnp.int32), seg_blocks[:-1, -1]])
    places = jnp.arange(STRETCH, dtype=jnp.int32)
    lower = places[:, None] >= places[None, :]

    def advance(state, pieces):
        x_block, b_block, c_block, dt_block, seg_block, prior = pieces
        logs = jnp.cumsum(dt_block * rate, axis=0)
        same = lower & (seg_block[:, None] == seg_block[None, :])
        spans = logs.T[:, :, None] - logs.T[:, None, :]
        factor = jnp.exp(jnp.where(same[None], spans, -1e30))
        scores = jnp.dot(c_block, b_block.T, precision=lax.Precision.HIGHEST)
        mixing = factor * scores[None] * dt_block.T[:, None, :]
        inside = jnp.einsum("htu,uhp->thp", mixing, x_block, precision=lax.Precision.HIGHEST)
        entering = jnp.exp(logs) * (seg_block == prior).astype(logs.dtype)[:, None]
        carried = (
            jnp.einsum("tn,hnp->thp", c_block, state, precision=lax.Precision.HIGHEST)
            * entering[:, :, None]
        )
        tail_mask = (seg_block == seg_block[-1]).astype(logs.dtype)[:, None]
        towards = jnp.exp(logs[-1][None, :] - logs) * dt_block * tail_mask
        fresh = jnp.einsum(
            "th,tn,thp->hnp", towards, b_block, x_block, precision=lax.Precision.HIGHEST
        )
        kept = jnp.exp(logs[-1]) * (seg_block[-1] == prior).astype(logs.dtype)
        return (fresh + kept[:, None, None] * state, inside + carried)

    initial = jnp.zeros((HEADS, STATE, HEAD_DIM), values.dtype)
    inputs = (
        values.reshape(number, STRETCH, HEADS, HEAD_DIM),
        bmat.reshape(number, STRETCH, STATE),
        cmat.reshape(number, STRETCH, STATE),
        steps_dt.reshape(number, STRETCH, HEADS),
        seg_blocks,
        before,
    )
    final_state, outputs = lax.scan(advance, initial, inputs)
    return outputs.reshape(rows, HEADS, HEAD_DIM)


def mixer(
    proj, dt_raw, conv_weight, conv_bias, dt_bias, a_log, d_skip, gain_out, lag_list, seq_ids
):
    rows = proj.shape[0]
    gate = proj[:, :INNER]
    conv_in = proj[:, INNER:]
    convolved = conv_bias + conv_weight[KERNEL - 1] * conv_in
    for lag in range(1, KERNEL):
        shifted = jnp.concatenate(
            [jnp.zeros((lag, conv_in.shape[1]), conv_in.dtype), conv_in[:-lag]]
        )
        convolved = convolved + conv_weight[KERNEL - 1 - lag] * shifted * lag_list[lag - 1]
    active = jax.nn.silu(convolved)
    values = active[:, :INNER].reshape(rows, HEADS, HEAD_DIM)
    bmat = active[:, INNER : INNER + STATE]
    cmat = active[:, INNER + STATE :]
    steps_dt = jax.nn.softplus(dt_raw + dt_bias)
    scanned = state_space(values, bmat, cmat, steps_dt, -jnp.exp(a_log), seq_ids)
    scanned = scanned + d_skip[None, :, None] * values
    gated = scanned.reshape(rows, INNER) * jax.nn.silu(gate)
    scale = lax.rsqrt(jnp.mean(gated * gated, axis=-1, keepdims=True) + EPS)
    return gated * scale * gain_out


def partial_mixer(masks, seq_ids):

    def apply_mixer(proj, dt_raw, conv_weight, conv_bias, dt_bias, a_log, d_skip, gain_out):
        return mixer(
            proj, dt_raw, conv_weight, conv_bias, dt_bias, a_log, d_skip, gain_out, masks, seq_ids
        )

    return apply_mixer


def block_pass(tokens, cotangent, seq_ids, weights, total):
    gain_in, w_main, w_dt, conv_w, conv_b, dt_bias, a_log, d_skip, gain_out, w_out = weights
    small = [
        piece.astype(jnp.float32) for piece in (conv_w, conv_b, dt_bias, a_log, d_skip, gain_out)
    ]
    inputs = tokens.astype(jnp.float32)
    normed_full, norm_back = jax.vjp(norm_in, inputs, gain_in.astype(jnp.float32))
    normed = normed_full.astype(jnp.bfloat16)
    proj = matmul(normed, w_main)
    dt_raw = matmul(normed, w_dt)
    masks = lag_masks(seq_ids)
    mixed_full, mixer_back = jax.vjp(partial_mixer(masks, seq_ids), proj, dt_raw, *small)
    hidden = mixed_full.astype(jnp.bfloat16)
    result = (inputs + matmul(hidden, w_out)).astype(jnp.bfloat16)
    live_cot = jnp.where(seq_ids[:, None] >= 0, cotangent, jnp.zeros_like(cotangent))
    grad_hidden = against(live_cot, w_out)
    backward = mixer_back(grad_hidden)
    grad_proj = backward[0].astype(jnp.bfloat16)
    grad_dt = backward[1].astype(jnp.bfloat16)
    grad_w_dt = over_rows(normed, grad_dt)
    grad_normed = against(grad_proj, w_main) + against(grad_dt, w_dt)
    grad_x, grad_gain = norm_back(grad_normed)
    grad_input = live_cot.astype(jnp.float32) + grad_x
    small_flat = jnp.concatenate([piece.reshape(-1) for piece in [grad_w_dt] + list(backward[2:])])
    small_flat = jnp.pad(small_flat, (0, ROWS_SMALL * LANES - small_flat.shape[0]))
    flat = pack_all(
        grad_gain.reshape(ROWS_GAIN, LANES),
        small_flat.reshape(ROWS_SMALL, LANES),
        normed,
        grad_proj,
        hidden,
        live_cot,
        total // LANES,
    )
    return (result, grad_input, flat)


def adamw(weight, first, second, grad, step_count):
    steps_done = step_count[0].astype(jnp.float32)
    first_new = BETA_ONE * first + (1.0 - BETA_ONE) * grad
    second_new = BETA_TWO * second + (1.0 - BETA_TWO) * grad * grad
    first_hat = first_new / (1.0 - jnp.power(BETA_ONE, steps_done))
    second_hat = second_new / (1.0 - jnp.power(BETA_TWO, steps_done))
    weight_new = weight - LEARN_RATE * (
        first_hat / (jnp.sqrt(second_hat) + ADAM_EPS) + WEIGHT_DECAY * weight
    )
    return (weight_new, first_new, second_new)


def per_device(tokens, cotangent, seq_ids, params, first_moment, second_moment, step_count):
    width = params.shape[0]
    rounded = params.astype(jnp.bfloat16)
    own = rounded.reshape(width // LANES, LANES)
    whole = gather_rows(own, lax.axis_size("shard"), lax.axis_size("dp"))
    weights = unpack(whole)
    result, grad_input, flat = block_pass(tokens, cotangent, seq_ids, weights, whole.size)
    owned = scatter_sum(flat, lax.axis_size("shard"), lax.axis_size("dp"), width // LANES)
    owned = owned.reshape(width)
    new_weight, new_first, new_second = adamw(
        params, first_moment, second_moment, owned, step_count
    )
    return (result, grad_input, owned, new_weight, new_first, new_second)


def solution(mesh):
    return jax.shard_map(
        per_device,
        mesh=mesh,
        in_specs=(
            P(("dp", "shard"), None),
            P(("dp", "shard"), None),
            P(("dp", "shard")),
            P(("dp", "shard")),
            P(("dp", "shard")),
            P(("dp", "shard")),
            P(),
        ),
        out_specs=(
            P(("dp", "shard"), None),
            P(("dp", "shard"), None),
            P(("dp", "shard")),
            P(("dp", "shard")),
            P(("dp", "shard")),
            P(("dp", "shard")),
        ),
        check_vma=False,
    )
```
